32 devices in a mesh: dp: 16 (over z, x, core), head: 2 (over y).
Axes of the slice: x: 2, y: 2, z: 4, core: 2. Of those that a mesh axis runs over, the one named last changes fastest.
Arguments:
- x_input: bfloat16 [2048, 8192], P('dp'), may hold values from -8 to 8
- wq_old: bfloat16 [8192, 1024], P('dp', 'head'), may hold values from -0.0625 to 0.0625
- wq_fresh: bfloat16 [8192, 256], P('dp', 'head'), may hold values from -0.0625 to 0.0625
- key_projection_weight: bfloat16 [8192, 256], P('dp', 'head'), may hold values from -0.0625 to 0.0625
- value_projection_weight: bfloat16 [8192, 256], P('dp', 'head'), may hold values from -0.0625 to 0.0625
- attention_output_gradient: bfloat16 [2048, 1280], P('dp', 'head'), may hold values from -6 to 6
- head_source: int32 [10], replicated, may hold values from 0 to 9, as said below
- doc_ids: int32 [2048], P('dp'), may hold values from 0 to 63, never falling along the last dimension, each value on 1 to 128 neighbouring positions
Outputs:
- attn_out: bfloat16 [2048, 1280], P('dp', 'head')
- x_grad: bfloat16 [2048, 8192], P('dp', 'head')
The draws below stay inside these ranges and needn't reach their ends.
Inputs may be any that keep to these rules, and one draw needn't show every extreme that they name: head_source is a permutation. There are shifts s_k and a permutation t of the 5 local indices, the same for every owner d, such that new head d * 5 + k takes candidate ((d - s_k) mod 2) * 5 + t_k; one owner takes at most 3 new head from any one former owner, and some pair reaches 3.
All inputs are finite; a program needn't handle non-finite values.
Results may differ from the reference program's by a relative error of at most 0.014.
The reference program's roundings to bfloat16 on the way count: a program that leaves them out, or rounds other values in their place, can miss the bound.
Values may be sent and summed in bfloat16 or wider, within the bound.
A program may use at most 64 MiB of HBM per device.

```python
import math
import jax
import jax.numpy as jnp
import numpy as np
from jax import lax

MODEL_DIMENSION = 8192
HEAD_SIZE = 128
GROUP = 5
OLD_DEV = 4
FRESH_DEV = 1
TOK_DEV = 128
TOKENS = 2048
KEY_VALUE_HEADS = 2
HQ = 10
HQ_OLD = 8
FRESH = 2
N_DP = 16
N_HEAD = 2


def draw_head_source(key, part):
    key_order, key_offset, key_taken = jax.random.split(jax.random.fold_in(key, 17), 3)
    order = jax.random.permutation(key_order, GROUP)
    offset = jax.random.randint(key_offset, (), 0, N_HEAD)
    shifts = (order + offset) % N_HEAD
    taken_index = jax.random.permutation(key_taken, GROUP)
    device = jnp.arange(N_HEAD)[:, None]
    source = (device - shifts[None, :]) % N_HEAD * GROUP + taken_index[None, :]
    return source.reshape(HQ).astype(jnp.int32)


def draw_x_input(key, part):
    key_values = jax.random.fold_in(jax.random.fold_in(key, 29), 0)
    entries = jax.random.truncated_normal(key_values, -6.0, 6.0, (TOKENS, MODEL_DIMENSION), jnp.float32)
    return entries.astype(jnp.bfloat16)


def block_scale(stream_key, dims, shards, smallest, high):
    def one(axis_at, blocks):
        draws = jax.random.uniform(jax.random.fold_in(jax.random.fold_in(stream_key, 6), axis_at), (blocks,), jnp.float32, smallest / len(shards), high / len(shards))
        return jnp.repeat(jnp.exp(draws), dims[axis_at] // blocks).reshape((-1,) + (1,) * (len(dims) - axis_at - 1))

    level = one(*shards[0])
    for cut in shards[1:]:
        level = level * one(*cut)
    return level


def profile(amount, total, limit, skew):
    weights = [(1 << 20) // math.isqrt(grade ** skew) + 1 for grade in range(2, amount + 1)]
    spare, counts = total - limit - (amount - 1), [1] * (amount - 1)
    while spare > 0:
        free = [i for i in range(amount - 1) if counts[i] < limit]
        whole, budget = sum([weights[i] for i in free]), spare
        for i in free:
            addition = min(limit - counts[i], max(1, budget * weights[i] // whole), spare)
            counts[i] = counts[i] + addition
            spare = spare - addition
    return np.array([limit] + counts)


def ragged_sizes(rng, amount, total, bound, lean):
    if amount == 2:
        one = jax.random.randint(rng, (), max(1, total - bound), min(bound, total - 1) + 1)
        return jnp.stack([one, total - one])
    lengths = jnp.asarray(profile(amount, total, bound, lean), jnp.int32)
    couples = (amount - 1) // 2
    source_of, sink = lengths[1:1 + 2 * couples:2], lengths[2:2 + 2 * couples:2]
    room = jnp.minimum(source_of - 1, bound - sink)
    passed = jax.random.randint(jax.random.fold_in(rng, 1), (couples,), 0, 1 << 20) % (room + 1)
    lengths = lengths.at[1:1 + 2 * couples:2].set(source_of - passed).at[2:2 + 2 * couples:2].set(sink + passed)
    return lengths[jax.random.permutation(jax.random.fold_in(rng, 2), amount)]


def scatter_about(stream_key, dims, deviation, most, shards=(), held_as=jnp.bfloat16):
    level = block_scale(stream_key, dims, shards, -0.22, 0.18) if shards else 1.0
    result = jax.random.normal(stream_key, dims, jnp.float32) * deviation * level
    return jnp.minimum(jnp.maximum(result, -most), most).astype(held_as)


def setup_inputs(seed: int = 0) -> dict:
    streams_of = jax.random.split(jax.random.key(seed), 9)
    return {
        "x_input": draw_x_input(jax.random.fold_in(streams_of[8], 71), 0),
        "wq_old": scatter_about(streams_of[1], (MODEL_DIMENSION, HQ_OLD * HEAD_SIZE), MODEL_DIMENSION ** -0.5, 0.0625, ((0, 16), (1, 2))),
        "wq_fresh": scatter_about(streams_of[2], (MODEL_DIMENSION, FRESH * HEAD_SIZE), MODEL_DIMENSION ** -0.5, 0.0625, ((0, 16), (1, 2))),
        "key_projection_weight": scatter_about(streams_of[3], (MODEL_DIMENSION, KEY_VALUE_HEADS * HEAD_SIZE), MODEL_DIMENSION ** -0.5, 0.0625, ((0, 16), (1, 2))),
        "value_projection_weight": scatter_about(streams_of[4], (MODEL_DIMENSION, KEY_VALUE_HEADS * HEAD_SIZE), MODEL_DIMENSION ** -0.5, 0.0625, ((0, 16), (1, 2))),
        "attention_output_gradient": scatter_about(streams_of[5], (TOKENS, HQ * HEAD_SIZE), 1.0, 6.0, ((0, 16), (1, 2))),
        "head_source": draw_head_source(jax.random.fold_in(streams_of[8], 71), 0),
        "doc_ids": jnp.searchsorted(jnp.cumsum(ragged_sizes(streams_of[7], 4 * N_DP, TOKENS, TOK_DEV, 1)), jnp.arange(TOKENS), side="right").astype(jnp.int32),
    }


theta_base = 500000.0
neg_large = -1e+30

def rotary_tables(length, head_width):
    half_dim = head_width // 2
    frequency = theta_base ** (-2.0 * jnp.arange(half_dim, dtype=jnp.float32) / head_width)
    angles = jnp.arange(length, dtype=jnp.float32)[:, None] * frequency[None, :]
    return (jnp.cos(angles), jnp.sin(angles))

def rotate(field, cosine, sine_table):
    half_dim = field.shape[-1] // 2
    lower_half = field[..., :half_dim]
    upper_half = field[..., half_dim:]
    cosine = cosine[:, None, :]
    sine_table = sine_table[:, None, :]
    return jnp.concatenate([lower_half * cosine - upper_half * sine_table, upper_half * cosine + lower_half * sine_table], axis=-1)

def rotate_back(field, cosine, sine_table):
    half_dim = field.shape[-1] // 2
    lower_half = field[..., :half_dim]
    upper_half = field[..., half_dim:]
    cosine = cosine[:, None, :]
    sine_table = sine_table[:, None, :]
    return jnp.concatenate([lower_half * cosine + upper_half * sine_table, upper_half * cosine - lower_half * sine_table], axis=-1)

def attention_pair(queries, key_rot, values, cotangent, doc_rows):
    length = queries.shape[0]
    scale_factor = 1.0 / math.sqrt(queries.shape[-1])
    query_f = queries.astype(jnp.float32)
    key_f = key_rot.astype(jnp.float32)
    value_f = values.astype(jnp.float32)
    cotan_f = cotangent.astype(jnp.float32)
    scores = jnp.einsum('qhd,kd->hqk', query_f, key_f) * scale_factor
    positions = jnp.arange(length)
    allowed = (positions[None, :] <= positions[:, None]) & (doc_rows[None, :] == doc_rows[:, None])
    scores = jnp.where(allowed[None], scores, neg_large)
    row_maximum = lax.optimization_barrier(jnp.max(scores, axis=-1, keepdims=True))
    weights = jnp.exp(scores - row_maximum)
    probability = weights / lax.optimization_barrier(jnp.sum(weights, axis=-1, keepdims=True))
    prob_b = probability.astype(jnp.bfloat16)
    prob_bf = prob_b.astype(jnp.float32)
    output = jnp.einsum('hqk,kd->qhd', prob_bf, value_f).astype(jnp.bfloat16)
    prob_grad = jnp.einsum('qhd,kd->hqk', cotan_f, value_f)
    centre = lax.optimization_barrier(jnp.sum(probability * prob_grad, axis=-1, keepdims=True))
    dscore = (probability * (prob_grad - centre) * scale_factor).astype(jnp.bfloat16).astype(jnp.float32)
    dquery = jnp.einsum('hqk,kd->qhd', dscore, key_f)
    key_grad = jnp.einsum('hqk,qhd->kd', dscore, query_f)
    dvalue = jnp.einsum('hqk,qhd->kd', prob_bf, cotan_f)
    return (output, dquery, key_grad, dvalue)

def reference(x_input, wq_old, wq_fresh, key_projection_weight, value_projection_weight, attention_output_gradient, head_source, doc_ids):
    model_width = x_input.shape[1]
    token_stream = x_input.shape[0]
    source = jnp.concatenate([wq_old.reshape(model_width, N_HEAD, OLD_DEV, HEAD_SIZE), wq_fresh.reshape(model_width, N_HEAD, FRESH_DEV, HEAD_SIZE)], axis=2).reshape(model_width, HQ, HEAD_SIZE)
    wq_new = jnp.take(source, head_source, axis=1).reshape(model_width, HQ * HEAD_SIZE)
    cosine, sine_table = rotary_tables(TOK_DEV, HEAD_SIZE)
    projected = jnp.dot(x_input, wq_new, preferred_element_type=jnp.float32).reshape(N_DP, TOK_DEV, HQ, HEAD_SIZE)
    queries = rotate(projected, cosine, sine_table).astype(jnp.bfloat16).reshape(N_DP, TOK_DEV, N_HEAD, GROUP, HEAD_SIZE)
    key_proj = jnp.dot(x_input, key_projection_weight, preferred_element_type=jnp.float32).reshape(N_DP, TOK_DEV, N_HEAD, HEAD_SIZE)
    key_rot = rotate(key_proj, cosine, sine_table).astype(jnp.bfloat16)
    values = jnp.dot(x_input, value_projection_weight, preferred_element_type=jnp.float32).astype(jnp.bfloat16).reshape(N_DP, TOK_DEV, N_HEAD, HEAD_SIZE)
    cotangent = attention_output_gradient.reshape(N_DP, TOK_DEV, N_HEAD, GROUP, HEAD_SIZE)
    doc_rows = doc_ids.reshape(N_DP, TOK_DEV)
    per_group = jax.vmap(attention_pair, in_axes=(1, 1, 1, 1, None), out_axes=(1, 1, 1, 1))
    per_sequence = jax.vmap(per_group, in_axes=(0, 0, 0, 0, 0), out_axes=(0, 0, 0, 0))
    output, dquery, key_grad, dvalue = per_sequence(queries, key_rot, values, cotangent, doc_rows)
    attn_out = output.reshape(token_stream, HQ * HEAD_SIZE)
    dquery = rotate_back(dquery.reshape(N_DP, TOK_DEV, HQ, HEAD_SIZE), cosine, sine_table).astype(jnp.bfloat16).reshape(token_stream, HQ * HEAD_SIZE)
    key_grad = rotate_back(key_grad, cosine, sine_table).astype(jnp.bfloat16).reshape(token_stream, N_HEAD * HEAD_SIZE)
    dvalue = dvalue.astype(jnp.bfloat16).reshape(token_stream, N_HEAD * HEAD_SIZE)
    summed = jnp.zeros((token_stream, model_width), jnp.float32)
    query_cols = GROUP * HEAD_SIZE
    for member in range(N_HEAD):
        q_lo = member * query_cols
        k_lo = member * HEAD_SIZE
        portion = jnp.dot(dquery[:, q_lo:q_lo + query_cols], wq_new[:, q_lo:q_lo + query_cols].T, preferred_element_type=jnp.float32)
        portion = portion + jnp.dot(key_grad[:, k_lo:k_lo + HEAD_SIZE], key_projection_weight[:, k_lo:k_lo + HEAD_SIZE].T, preferred_element_type=jnp.float32)
        portion = portion + jnp.dot(dvalue[:, k_lo:k_lo + HEAD_SIZE], value_projection_weight[:, k_lo:k_lo + HEAD_SIZE].T, preferred_element_type=jnp.float32)
        rounded = lax.optimization_barrier(portion.astype(jnp.bfloat16))
        summed = summed + rounded.astype(jnp.float32)
    return (attn_out, summed.astype(jnp.bfloat16))
```

```python
import functools
import math

import jax
import jax.numpy as jnp
import numpy as np
from jax import lax
from jax.experimental import pallas as pl
from jax.experimental.pallas import tpu as pltpu
from jax.sharding import PartitionSpec as P

theta_base = 500000.0
neg_large = -1e30
MESH = pl.DeviceIdType.MESH


def rotary_tables(length, width):
    half = width // 2
    frequency = theta_base ** (-2.0 * np.arange(half, dtype=np.float64) / width)
    angles = np.arange(length, dtype=np.float64)[:, None] * frequency[None, :]
    cosine, sine = np.cos(angles), np.sin(angles)
    return (
        np.concatenate([cosine, cosine], axis=1).astype(np.float32),
        np.concatenate([-sine, sine], axis=1).astype(np.float32),
    )


def dot(a, b, ca, cb):
    return lax.dot_general(
        a, b, (((ca,), (cb,)), ((), ())), preferred_element_type=jnp.float32
    )


def kernel(
    n_dp, n_head, group, ways,
    src_ref, doc_ref, cos_ref, sin_ref, x_hbm, old_hbm, fresh_hbm, k_hbm, v_hbm, g_hbm,
    out_ref, grad_ref,
    x_ref, own_ref, g_ref, wq, wkv, parcel, arrived, accq, acckv, dq_ref, dkv_ref,
    psend, precv,
    in_sem, rs, rr, cs, cr, hs, hr, ps, pr,
):
    me, head = lax.axis_index("dp"), lax.axis_index("head")
    rows, hd = k_hbm.shape
    length = x_ref.shape[0]
    lanes = 2
    m = n_dp // lanes
    core, chip = me % lanes, me // lanes
    side, level = chip % 2, chip // 2
    pos = (1 - side) * level + side * (m - 1 - level)
    piece = rows // ways
    capacity = parcel.shape[1]
    signs = (1, -1)[:ways]
    bufs = (wkv, wq)

    def index_of(p, lane):
        p = (p + 2 * m) % m
        far = p // (m // 2)
        return ((1 - far) * 2 * p + far * (2 * (m - 1 - p) + 1)) * lanes + lane

    right, left = index_of(pos + 1, core), index_of(pos - 1, core)
    targets = (right, left)[:ways]
    partner = index_of(pos, 1 - core)

    loads = [
        pltpu.make_async_copy(k_hbm, wkv.at[me, :, pl.ds(0, hd)], in_sem.at[0]),
        pltpu.make_async_copy(v_hbm, wkv.at[me, :, pl.ds(hd, hd)], in_sem.at[1]),
        pltpu.make_async_copy(old_hbm, own_ref.at[:, pl.ds(0, (group - 1) * hd)], in_sem.at[2]),
        pltpu.make_async_copy(fresh_hbm, own_ref.at[:, pl.ds((group - 1) * hd, hd)], in_sem.at[3]),
        pltpu.make_async_copy(x_hbm, x_ref, in_sem.at[4]),
        pltpu.make_async_copy(g_hbm, g_ref, in_sem.at[5]),
    ]
    for load in loads:
        load.start()

    barrier = pltpu.get_barrier_semaphore()
    peers = [(right, head), (left, head), (partner, head)]
    peers += [(me, (head + j) % n_head) for j in range(1, n_head)]
    for peer in peers:
        pl.semaphore_signal(barrier, inc=1, device_id=peer, device_id_type=MESH)

    def part_of(p, w, owner):
        return bufs[p].at[owner, pl.ds(w * piece, piece)]

    def ring(p, w, s):
        ref = part_of(p, w, index_of(pos - signs[w] * s, core))
        return pltpu.make_async_remote_copy(
            ref, ref, rs.at[w * 2 + p, s], rr.at[w * 2 + p, s],
            device_id=(targets[w], head), device_id_type=MESH)

    def ring_in(p, w, s):
        ref = part_of(p, w, index_of(pos - signs[w] * (s + 1), core))
        return pltpu.make_async_remote_copy(
            ref, ref, rs.at[w * 2 + p, s], rr.at[w * 2 + p, s],
            device_id=(targets[w], head), device_id_type=MESH)

    def across(p, w, s, lane):
        ref = part_of(p, w, index_of(pos - signs[w] * s, lane))
        return pltpu.make_async_remote_copy(
            ref, ref, cs.at[w * 2 + p, s], cr.at[w * 2 + p, s],
            device_id=(partner, head), device_id_type=MESH)

    def relay(j):
        return pltpu.make_async_remote_copy(
            parcel.at[j - 1], arrived.at[j - 1], hs.at[j - 1], hr.at[j - 1],
            device_id=(me, (head + j) % n_head), device_id_type=MESH)

    shift = [(n_head - src_ref[k] // group) % n_head for k in range(group)]
    taken = [src_ref[k] % group for k in range(group)]
    slot = [
        sum([(shift[l] == shift[k]).astype(jnp.int32) for l in range(k)], jnp.int32(0))
        for k in range(group)
    ]

    def flag(cond):
        return jnp.where(cond, 1.0, 0.0).astype(jnp.float32)

    for load in loads[2:4]:
        load.wait()
    for j in range(1, n_head):
        for c in range(capacity):
            total = jnp.zeros((rows, hd), jnp.float32)
            for c_m in range(group):
                weight = sum(
                    [flag((shift[k] == j) & (slot[k] == c) & (taken[k] == c_m)) for k in range(group)],
                    jnp.float32(0))
                total = total + own_ref[:, c_m * hd:(c_m + 1) * hd].astype(jnp.float32) * weight
            parcel[j - 1, c] = total.astype(jnp.bfloat16)
    for load in loads[:2]:
        load.wait()
    pl.semaphore_wait(barrier, len(peers))
    for j in range(1, n_head):
        relay(j).start()
    for w in range(ways):
        ring(0, w, 0).start()
    for w in range(ways):
        across(0, w, 0, core).start()

    for load in loads[4:]:
        load.wait()
    accq[...] = jnp.zeros_like(accq)
    acckv[...] = jnp.zeros_like(acckv)

    def add(p, w, owner):
        xs = x_ref[:, pl.ds(pl.multiple_of(owner * rows + w * piece, 128), piece)]
        acc = (acckv, accq)[p]
        acc[...] += dot(xs, bufs[p][owner, pl.ds(w * piece, piece), :], 1, 0)

    for j in range(1, n_head):
        relay(j).wait_recv()
    for k in range(group):
        total = jnp.zeros((rows, hd), jnp.float32)
        for c_m in range(group):
            weight = flag((shift[k] == 0) & (taken[k] == c_m))
            total = total + own_ref[:, c_m * hd:(c_m + 1) * hd].astype(jnp.float32) * weight
        for j in range(1, n_head):
            for c in range(capacity):
                weight = flag((shift[k] == j) & (slot[k] == c))
                total = total + arrived[j - 1, c].astype(jnp.float32) * weight
        wq[me, :, k * hd:(k + 1) * hd] = total.astype(jnp.bfloat16)
    for w in range(ways):
        ring(1, w, 0).start()
    for w in range(ways):
        across(1, w, 0, core).start()
    for w in range(ways):
        for p in range(2):
            add(p, w, me)

    def step(s, carry):
        for p in range(2):
            for w in range(ways):
                ring_in(p, w, s - 1).wait_recv()

                @pl.when(s < m - 1)
                def _():
                    ring(p, w, s).start()

                across(p, w, s, core).start()
        for w in range(ways):
            for p in range(2):
                add(p, w, index_of(pos - signs[w] * s, core))
        for w in range(ways):
            for p in range(2):
                across(p, w, s - 1, 1 - core).wait_recv()
        for w in range(ways):
            for p in range(2):
                add(p, w, index_of(pos - signs[w] * (s - 1), 1 - core))
        return carry

    lax.fori_loop(1, m, step, 0)
    for w in range(ways):
        for p in range(2):
            across(p, w, m - 1, 1 - core).wait_recv()
            add(p, w, index_of(pos - signs[w] * (m - 1), 1 - core))

    scale = 1.0 / math.sqrt(hd)
    cosine, sine = cos_ref[...], sin_ref[...]

    def rotate(f):
        return f * cosine + pltpu.roll(f, hd // 2, 1) * sine

    def rotate_back(f):
        return f * cosine - pltpu.roll(f, hd // 2, 1) * sine

    docs = jnp.broadcast_to(doc_ref[...].astype(jnp.float32), (length, length))
    at_key = lax.broadcasted_iota(jnp.int32, (length, length), 1)
    at_query = lax.broadcasted_iota(jnp.int32, (length, length), 0)
    allowed = (at_key <= at_query) & (docs == docs.T)
    key = rotate(acckv[:, :hd]).astype(jnp.bfloat16)
    value = acckv[:, hd:].astype(jnp.bfloat16)
    dkey = jnp.zeros((length, hd), jnp.float32)
    dvalue = jnp.zeros((length, hd), jnp.float32)
    for k in range(group):
        cols = slice(k * hd, (k + 1) * hd)
        query = rotate(accq[:, cols]).astype(jnp.bfloat16)
        given = g_ref[:, cols]
        scores = jnp.where(allowed, dot(query, key, 1, 1) * scale, neg_large)
        weights = jnp.exp(scores - jnp.max(scores, axis=-1, keepdims=True))
        probs = weights / jnp.sum(weights, axis=-1, keepdims=True)
        probs_b = probs.astype(jnp.bfloat16)
        out_ref[:, cols] = dot(probs_b, value, 1, 0).astype(jnp.bfloat16)
        prob_grad = dot(given, value, 1, 1)
        centre = jnp.sum(probs * prob_grad, axis=-1, keepdims=True)
        dscore = (probs * (prob_grad - centre) * scale).astype(jnp.bfloat16)
        dq_ref[:, cols] = rotate_back(dot(dscore, key, 1, 0)).astype(jnp.bfloat16)
        dkey = dkey + dot(dscore, query, 0, 0)
        dvalue = dvalue + dot(probs_b, given, 0, 0)
    dkv_ref[:, :hd] = rotate_back(dkey).astype(jnp.bfloat16)
    dkv_ref[:, hd:] = dvalue.astype(jnp.bfloat16)

    chunks = n_dp // n_head

    def partial(owner):
        return (dot(dq_ref[...], wq[owner], 1, 1) + dot(dkv_ref[...], wkv[owner], 1, 1)).astype(
            jnp.bfloat16)

    def share(j, i):
        return pltpu.make_async_remote_copy(
            psend.at[j - 1, i], precv.at[j - 1, i], ps.at[j - 1, i], pr.at[j - 1, i],
            device_id=(me, (head + j) % n_head), device_id_type=MESH)

    for j in range(1, n_head):
        def send_chunk(i, carry):
            psend[j - 1, i] = partial(((head + j) % n_head) * chunks + i)
            share(j, i).start()
            return carry

        lax.fori_loop(0, chunks, send_chunk, 0)

    def own_chunk(i, carry):
        cols = pl.ds(pl.multiple_of(i * rows, 128), rows)
        grad_ref[:, cols] = partial(head * chunks + i)
        return carry

    lax.fori_loop(0, chunks, own_chunk, 0)

    def finish(i, carry):
        cols = pl.ds(pl.multiple_of(i * rows, 128), rows)
        total = grad_ref[:, cols].astype(jnp.float32)
        for j in range(1, n_head):
            share(j, i).wait_recv()
            total = total + precv[j - 1, i].astype(jnp.float32)
        grad_ref[:, cols] = total.astype(jnp.bfloat16)
        return carry

    lax.fori_loop(0, chunks, finish, 0)

    def drain(s, carry):
        for p in range(2):
            for w in range(ways):
                @pl.when(s < m - 1)
                def _():
                    ring(p, w, s).wait_send()

                across(p, w, s, core).wait_send()
        return carry

    lax.fori_loop(0, m, drain, 0)
    for j in range(1, n_head):
        relay(j).wait_send()

        def drain_share(i, carry):
            share(j, i).wait_send()
            return carry

        lax.fori_loop(0, chunks, drain_share, 0)


def solution(mesh):
    n_dp, n_head = mesh.shape["dp"], mesh.shape["head"]

    def local(x, old, fresh, wk, wv, g, head_source, doc_ids):
        length, width = x.shape
        rows, hd = wk.shape
        group = g.shape[1] // hd
        ways = 2 if rows % 256 == 0 else 1
        m = n_dp // 2
        capacity = (group + n_head - 1) // n_head
        chunks = n_dp // n_head
        cosine, sine = rotary_tables(length, hd)
        bf, f32 = jnp.bfloat16, jnp.float32
        vm = pl.BlockSpec(memory_space=pltpu.VMEM)
        anyspace = pl.BlockSpec(memory_space=pl.ANY)
        dma = pltpu.SemaphoreType.DMA
        return pl.pallas_call(
            functools.partial(kernel, n_dp, n_head, group, ways),
            out_shape=(
                jax.ShapeDtypeStruct((length, group * hd), bf),
                jax.ShapeDtypeStruct((length, width // n_head), bf),
            ),
            in_specs=[pl.BlockSpec(memory_space=pltpu.SMEM), vm, vm, vm] + [anyspace] * 6,
            out_specs=(vm, vm),
            scratch_shapes=[
                pltpu.VMEM((length, width), bf),
                pltpu.VMEM((rows, group * hd), bf),
                pltpu.VMEM((length, group * hd), bf),
                pltpu.VMEM((n_dp, rows, group * hd), bf),
                pltpu.VMEM((n_dp, rows, 2 * hd), bf),
                pltpu.VMEM((n_head - 1, capacity, rows, hd), bf),
                pltpu.VMEM((n_head - 1, capacity, rows, hd), bf),
                pltpu.VMEM((length, group * hd), f32),
                pltpu.VMEM((length, 2 * hd), f32),
                pltpu.VMEM((length, group * hd), bf),
                pltpu.VMEM((length, 2 * hd), bf),
                pltpu.VMEM((n_head - 1, chunks, length, rows), bf),
                pltpu.VMEM((n_head - 1, chunks, length, rows), bf),
                dma((6,)),
                dma((2 * ways, m)),
                dma((2 * ways, m)),
                dma((2 * ways, m)),
                dma((2 * ways, m)),
                dma((n_head - 1,)),
                dma((n_head - 1,)),
                dma((n_head - 1, chunks)),
                dma((n_head - 1, chunks)),
            ],
            compiler_params=pltpu.CompilerParams(
                collective_id=0, has_side_effects=True, vmem_limit_bytes=50 * 1024 * 1024),
        )(head_source, doc_ids.reshape(1, -1), cosine, sine, x, old, fresh, wk, wv, g)

    in_specs = (
        P("dp", None), P("dp", "head"), P("dp", "head"), P("dp", "head"),
        P("dp", "head"), P("dp", "head"), P(), P("dp"),
    )
    return jax.shard_map(
        local, mesh=mesh, in_specs=in_specs,
        out_specs=(P("dp", "head"), P("dp", "head")), check_vma=False)
```

```python
import functools
import math

import jax
import jax.numpy as jnp
import numpy as np
from jax import lax
from jax.experimental import pallas as pl
from jax.experimental.pallas import tpu as pltpu
from jax.sharding import PartitionSpec as P

theta_base = 500000.0
neg_large = -1e30
MESH = pl.DeviceIdType.MESH


def rotary_tables(length, width):
    half = width // 2
    frequency = theta_base ** (-2.0 * np.arange(half, dtype=np.float64) / width)
    angles = np.arange(length, dtype=np.float64)[:, None] * frequency[None, :]
    cosine, sine = np.cos(angles), np.sin(angles)
    return (
        np.concatenate([cosine, cosine], axis=1).astype(np.float32),
        np.concatenate([-sine, sine], axis=1).astype(np.float32),
    )


def dot(a, b, ca, cb):
    return lax.dot_general(
        a, b, (((ca,), (cb,)), ((), ())), preferred_element_type=jnp.float32
    )


def kernel(
    n_dp, n_head, group, ways,
    src_ref, doc_ref, cos_ref, sin_ref, x_hbm, old_hbm, fresh_hbm, k_hbm, v_hbm, g_hbm,
    out_ref, grad_ref,
    x_ref, own_ref, g_ref, wq, wkv, parcel, arrived, accq, acckv, dq_ref, dkv_ref,
    psend, precv,
    in_sem, rs, rr, cs, cr, hs, hr, ps, pr,
):
    me, head = lax.axis_index("dp"), lax.axis_index("head")
    rows, hd = k_hbm.shape
    length = x_ref.shape[0]
    lanes = 2
    m = n_dp // lanes
    core, chip = me % lanes, me // lanes
    side, level = chip % 2, chip // 2
    pos = (1 - side) * level + side * (m - 1 - level)
    piece = rows // ways
    sub = piece // 2
    lead = min(2, m - 2)
    parts = 3
    capacity = parcel.shape[2]
    signs = (1, -1)[:ways]
    bufs = (wkv, wq)
    spans = ((0, piece), (0, sub), (sub, sub))

    def index_of(p, lane):
        p = (p + 2 * m) % m
        far = p // (m // 2)
        return ((1 - far) * 2 * p + far * (2 * (m - 1 - p) + 1)) * lanes + lane

    right, left = index_of(pos + 1, core), index_of(pos - 1, core)
    targets = (right, left)[:ways]
    partner = index_of(pos, 1 - core)

    loads = [
        pltpu.make_async_copy(k_hbm, wkv.at[me, :, pl.ds(0, hd)], in_sem.at[0]),
        pltpu.make_async_copy(v_hbm, wkv.at[me, :, pl.ds(hd, hd)], in_sem.at[1]),
        pltpu.make_async_copy(old_hbm, own_ref.at[:, pl.ds(0, (group - 1) * hd)], in_sem.at[2]),
        pltpu.make_async_copy(fresh_hbm, own_ref.at[:, pl.ds((group - 1) * hd, hd)], in_sem.at[3]),
        pltpu.make_async_copy(x_hbm, x_ref, in_sem.at[4]),
        pltpu.make_async_copy(g_hbm, g_ref, in_sem.at[5]),
    ]
    for load in loads:
        load.start()

    barrier = pltpu.get_barrier_semaphore()
    peers = [(right, head), (left, head), (partner, head)]
    peers += [(me, (head + j) % n_head) for j in range(1, n_head)]
    for peer in peers:
        pl.semaphore_signal(barrier, inc=1, device_id=peer, device_id_type=MESH)

    def part_of(p, w, owner):
        first, count = spans[p]
        return bufs[min(p, 1)].at[owner, pl.ds(w * piece + first, count)]

    def ring(p, w, s):
        ref = part_of(p, w, index_of(pos - signs[w] * s, core))
        return pltpu.make_async_remote_copy(
            ref, ref, rs.at[w * parts + p, s], rr.at[w * parts + p, s],
            device_id=(targets[w], head), device_id_type=MESH)

    def ring_in(p, w, s):
        ref = part_of(p, w, index_of(pos - signs[w] * (s + 1), core))
        return pltpu.make_async_remote_copy(
            ref, ref, rs.at[w * parts + p, s], rr.at[w * parts + p, s],
            device_id=(targets[w], head), device_id_type=MESH)

    def across(p, w, s, lane):
        ref = part_of(p, w, index_of(pos - signs[w] * s, lane))
        return pltpu.make_async_remote_copy(
            ref, ref, cs.at[w * parts + p, s], cr.at[w * parts + p, s],
            device_id=(partner, head), device_id_type=MESH)

    def relay(u, j):
        return pltpu.make_async_remote_copy(
            parcel.at[u, j - 1], arrived.at[u, j - 1], hs.at[u, j - 1], hr.at[u, j - 1],
            device_id=(me, (head + j) % n_head), device_id_type=MESH)

    shift = [(n_head - src_ref[k] // group) % n_head for k in range(group)]
    taken = [src_ref[k] % group for k in range(group)]
    slot = [
        sum([(shift[l] == shift[k]).astype(jnp.int32) for l in range(k)], jnp.int32(0))
        for k in range(group)
    ]

    def flag(cond):
        return jnp.where(cond, 1.0, 0.0).astype(jnp.float32)

    units = [w * 2 + half for half in range(2) for w in range(ways)]

    def weigh(u, weights):
        total = jnp.zeros((sub, hd), jnp.float32)
        for c_m in range(group):
            block = own_ref[u * sub:(u + 1) * sub, c_m * hd:(c_m + 1) * hd]
            total = total + block.astype(jnp.float32) * weights[c_m]
        return total.astype(jnp.bfloat16)

    for load in loads[:2]:
        load.wait()
    pl.semaphore_wait(barrier, len(peers))
    for w in range(ways):
        ring(0, w, 0).start()
    for w in range(ways):
        across(0, w, 0, core).start()
    for load in loads[2:4]:
        load.wait()
    for u in units:
        for j in range(1, n_head):
            for c in range(capacity):
                weights = [
                    sum([flag((shift[k] == j) & (slot[k] == c) & (taken[k] == c_m))
                         for k in range(group)], jnp.float32(0))
                    for c_m in range(group)
                ]
                parcel[u, j - 1, c] = weigh(u, weights)
            relay(u, j).start()
    for k in range(group):
        weights = [flag((shift[k] == 0) & (taken[k] == c_m)) for c_m in range(group)]
        for u in units:
            wq[me, u * sub:(u + 1) * sub, k * hd:(k + 1) * hd] = weigh(u, weights)
    for load in loads[4:]:
        load.wait()
    accq[...] = jnp.zeros_like(accq)
    acckv[...] = jnp.zeros_like(acckv)

    def add(p, w, owner):
        xs = x_ref[:, pl.ds(pl.multiple_of(owner * rows + w * piece, 128), piece)]
        acc = (acckv, accq)[p]
        acc[...] += dot(xs, bufs[p][owner, pl.ds(w * piece, piece), :], 1, 0)

    def pass_on(p, w, s):
        ring_in(p, w, s - 1).wait_recv()

        @pl.when(s < m - 1)
        def _():
            ring(p, w, s).start()

        across(p, w, s, core).start()

    def unit_out(u):
        block = pl.ds(u * sub, sub)
        for j in range(1, n_head):
            relay(u, j).wait_recv()
        for k in range(group):
            cols = slice(k * hd, (k + 1) * hd)
            total = wq[me, block, cols].astype(jnp.float32)
            for j in range(1, n_head):
                for c in range(capacity):
                    weight = flag((shift[k] == j) & (slot[k] == c))
                    total = total + arrived[u, j - 1, c].astype(jnp.float32) * weight
            wq[me, block, cols] = total.astype(jnp.bfloat16)
        ring(1 + u % 2, u // 2, 0).start()
        across(1 + u % 2, u // 2, 0, core).start()

    for w in range(ways):
        add(0, w, me)
    for u in units[:ways]:
        unit_out(u)
    for s in range(1, lead + 1):
        for w in range(ways):
            pass_on(0, w, s)
        if s == 1:
            for u in units[ways:]:
                unit_out(u)
    for w in range(ways):
        add(1, w, me)

    def step(s, carry):
        @pl.when(s + lead < m)
        def _():
            for w in range(ways):
                pass_on(0, w, s + lead)

        for p in range(1, parts):
            for w in range(ways):
                pass_on(p, w, s)
        for w in range(ways):
            for p in range(2):
                add(p, w, index_of(pos - signs[w] * s, core))
        for w in range(ways):
            for p in range(parts):
                across(p, w, s - 1, 1 - core).wait_recv()
        for w in range(ways):
            for p in range(2):
                add(p, w, index_of(pos - signs[w] * (s - 1), 1 - core))
        return carry

    lax.fori_loop(1, m, step, 0)
    for w in range(ways):
        for p in range(parts):
            across(p, w, m - 1, 1 - core).wait_recv()
        for p in range(2):
            add(p, w, index_of(pos - signs[w] * (m - 1), 1 - core))

    scale = 1.0 / math.sqrt(hd)
    cosine, sine = cos_ref[...], sin_ref[...]

    def rotate(f):
        return f * cosine + pltpu.roll(f, hd // 2, 1) * sine

    def rotate_back(f):
        return f * cosine - pltpu.roll(f, hd // 2, 1) * sine

    docs = jnp.broadcast_to(doc_ref[...].astype(jnp.float32), (length, length))
    at_key = lax.broadcasted_iota(jnp.int32, (length, length), 1)
    at_query = lax.broadcasted_iota(jnp.int32, (length, length), 0)
    allowed = (at_key <= at_query) & (docs == docs.T)
    key = rotate(acckv[:, :hd]).astype(jnp.bfloat16)
    value = acckv[:, hd:].astype(jnp.bfloat16)
    dkey = jnp.zeros((length, hd), jnp.float32)
    dvalue = jnp.zeros((length, hd), jnp.float32)
    for k in range(group):
        cols = slice(k * hd, (k + 1) * hd)
        query = rotate(accq[:, cols]).astype(jnp.bfloat16)
        given = g_ref[:, cols]
        scores = jnp.where(allowed, dot(query, key, 1, 1) * scale, neg_large)
        weights = jnp.exp(scores - jnp.max(scores, axis=-1, keepdims=True))
        probs = weights / jnp.sum(weights, axis=-1, keepdims=True)
        probs_b = probs.astype(jnp.bfloat16)
        out_ref[:, cols] = dot(probs_b, value, 1, 0).astype(jnp.bfloat16)
        prob_grad = dot(given, value, 1, 1)
        centre = jnp.sum(probs * prob_grad, axis=-1, keepdims=True)
        dscore = (probs * (prob_grad - centre) * scale).astype(jnp.bfloat16)
        dq_ref[:, cols] = rotate_back(dot(dscore, key, 1, 0)).astype(jnp.bfloat16)
        dkey = dkey + dot(dscore, query, 0, 0)
        dvalue = dvalue + dot(probs_b, given, 0, 0)
    dkv_ref[:, :hd] = rotate_back(dkey).astype(jnp.bfloat16)
    dkv_ref[:, hd:] = dvalue.astype(jnp.bfloat16)

    chunks = n_dp // n_head

    def partial(owner):
        return (dot(dq_ref[...], wq[owner], 1, 1) + dot(dkv_ref[...], wkv[owner], 1, 1)).astype(
            jnp.bfloat16)

    def share(j, i):
        return pltpu.make_async_remote_copy(
            psend.at[j - 1, i], precv.at[j - 1, i], ps.at[j - 1, i], pr.at[j - 1, i],
            device_id=(me, (head + j) % n_head), device_id_type=MESH)

    for j in range(1, n_head):
        def send_chunk(i, carry):
            psend[j - 1, i] = partial(((head + j) % n_head) * chunks + i)
            share(j, i).start()
            return carry

        lax.fori_loop(0, chunks, send_chunk, 0)

    def own_chunk(i, carry):
        cols = pl.ds(pl.multiple_of(i * rows, 128), rows)
        grad_ref[:, cols] = partial(head * chunks + i)
        return carry

    lax.fori_loop(0, chunks, own_chunk, 0)

    def finish(i, carry):
        cols = pl.ds(pl.multiple_of(i * rows, 128), rows)
        total = grad_ref[:, cols].astype(jnp.float32)
        for j in range(1, n_head):
            share(j, i).wait_recv()
            total = total + precv[j - 1, i].astype(jnp.float32)
        grad_ref[:, cols] = total.astype(jnp.bfloat16)
        return carry

    lax.fori_loop(0, chunks, finish, 0)

    def drain(s, carry):
        for p in range(parts):
            for w in range(ways):
                @pl.when(s < m - 1)
                def _():
                    ring(p, w, s).wait_send()

                across(p, w, s, core).wait_send()
        return carry

    lax.fori_loop(0, m, drain, 0)
    for j in range(1, n_head):
        for u in units:
            relay(u, j).wait_send()

        def drain_share(i, carry):
            share(j, i).wait_send()
            return carry

        lax.fori_loop(0, chunks, drain_share, 0)


def solution(mesh):
    n_dp, n_head = mesh.shape["dp"], mesh.shape["head"]

    def local(x, old, fresh, wk, wv, g, head_source, doc_ids):
        length, width = x.shape
        rows, hd = wk.shape
        group = g.shape[1] // hd
        ways = 2 if rows % 256 == 0 else 1
        m = n_dp // 2
        capacity = (group + n_head - 1) // n_head
        chunks = n_dp // n_head
        cosine, sine = rotary_tables(length, hd)
        bf, f32 = jnp.bfloat16, jnp.float32
        vm = pl.BlockSpec(memory_space=pltpu.VMEM)
        anyspace = pl.BlockSpec(memory_space=pl.ANY)
        dma = pltpu.SemaphoreType.DMA
        return pl.pallas_call(
            functools.partial(kernel, n_dp, n_head, group, ways),
            out_shape=(
                jax.ShapeDtypeStruct((length, group * hd), bf),
                jax.ShapeDtypeStruct((length, width // n_head), bf),
            ),
            in_specs=[pl.BlockSpec(memory_space=pltpu.SMEM), vm, vm, vm] + [anyspace] * 6,
            out_specs=(vm, vm),
            scratch_shapes=[
                pltpu.VMEM((length, width), bf),
                pltpu.VMEM((rows, group * hd), bf),
                pltpu.VMEM((length, group * hd), bf),
                pltpu.VMEM((n_dp, rows, group * hd), bf),
                pltpu.VMEM((n_dp, rows, 2 * hd), bf),
                pltpu.VMEM((2 * ways, n_head - 1, capacity, rows // (2 * ways), hd), bf),
                pltpu.VMEM((2 * ways, n_head - 1, capacity, rows // (2 * ways), hd), bf),
                pltpu.VMEM((length, group * hd), f32),
                pltpu.VMEM((length, 2 * hd), f32),
                pltpu.VMEM((length, group * hd), bf),
                pltpu.VMEM((length, 2 * hd), bf),
                pltpu.VMEM((n_head - 1, chunks, length, rows), bf),
                pltpu.VMEM((n_head - 1, chunks, length, rows), bf),
                dma((6,)),
                dma((3 * ways, m)),
                dma((3 * ways, m)),
                dma((3 * ways, m)),
                dma((3 * ways, m)),
                dma((2 * ways, n_head - 1)),
                dma((2 * ways, n_head - 1)),
                dma((n_head - 1, chunks)),
                dma((n_head - 1, chunks)),
            ],
            compiler_params=pltpu.CompilerParams(
                collective_id=0, has_side_effects=True, vmem_limit_bytes=50 * 1024 * 1024),
        )(head_source, doc_ids.reshape(1, -1), cosine, sine, x, old, fresh, wk, wv, g)

    in_specs = (
        P("dp", None), P("dp", "head"), P("dp", "head"), P("dp", "head"),
        P("dp", "head"), P("dp", "head"), P(), P("dp"),
    )
    return jax.shard_map(
        local, mesh=mesh, in_specs=in_specs,
        out_specs=(P("dp", "head"), P("dp", "head")), check_vma=False)
```

```python
import functools
import math

import jax
import jax.numpy as jnp
import numpy as np
from jax import lax
from jax.experimental import pallas as pl
from jax.experimental.pallas import tpu as pltpu
from jax.sharding import PartitionSpec as P

theta_base = 500000.0
neg_large = -1e30
MESH = pl.DeviceIdType.MESH


def rotary_tables(length, width):
    half = width // 2
    frequency = theta_base ** (-2.0 * np.arange(half, dtype=np.float64) / width)
    angles = np.arange(length, dtype=np.float64)[:, None] * frequency[None, :]
    cosine, sine = np.cos(angles), np.sin(angles)
    return (
        np.concatenate([cosine, cosine], axis=1).astype(np.float32),
        np.concatenate([-sine, sine], axis=1).astype(np.float32),
    )


def dot(a, b, ca, cb):
    return lax.dot_general(
        a, b, (((ca,), (cb,)), ((), ())), preferred_element_type=jnp.float32
    )


def kernel(
    n_dp, n_head, group, ways,
    src_ref, doc_hbm, cos_hbm, sin_hbm, x_hbm, old_hbm, fresh_hbm, k_hbm, v_hbm, g_hbm,
    out_ref, grad_ref,
    doc_ref, cos_ref, sin_ref, x_ref, own_ref, g_ref, wq, wkv, parcel, arrived, accq, acckv, dq_ref, dkv_ref,
    psend, precv,
    in_sem, rs, rr, cs, cr, hs, hr, ps, pr,
):
    me, head = lax.axis_index("dp"), lax.axis_index("head")
    rows, hd = k_hbm.shape
    length = x_ref.shape[0]
    lanes = 2
    m = n_dp // lanes
    core, chip = me % lanes, me // lanes
    side, level = chip % 2, chip // 2
    pos = (1 - side) * level + side * (m - 1 - level)
    piece = rows // ways
    sub = piece // 2
    lead = min(2, m - 2)
    parts = 3
    capacity = parcel.shape[2]
    signs = (1, -1)[:ways]
    bufs = (wkv, wq)
    spans = ((0, piece), (0, sub), (sub, sub))

    def index_of(p, lane):
        p = (p + 2 * m) % m
        far = p // (m // 2)
        return ((1 - far) * 2 * p + far * (2 * (m - 1 - p) + 1)) * lanes + lane

    right, left = index_of(pos + 1, core), index_of(pos - 1, core)
    targets = (right, left)[:ways]
    partner = index_of(pos, 1 - core)

    loads = [
        pltpu.make_async_copy(k_hbm, wkv.at[me, :, pl.ds(0, hd)], in_sem.at[0]),
        pltpu.make_async_copy(v_hbm, wkv.at[me, :, pl.ds(hd, hd)], in_sem.at[1]),
        pltpu.make_async_copy(old_hbm, own_ref.at[:, pl.ds(0, (group - 1) * hd)], in_sem.at[2]),
        pltpu.make_async_copy(fresh_hbm, own_ref.at[:, pl.ds((group - 1) * hd, hd)], in_sem.at[3]),
        pltpu.make_async_copy(x_hbm, x_ref, in_sem.at[4]),
        pltpu.make_async_copy(g_hbm, g_ref, in_sem.at[5]),
        pltpu.make_async_copy(doc_hbm, doc_ref, in_sem.at[6]),
        pltpu.make_async_copy(cos_hbm, cos_ref, in_sem.at[7]),
        pltpu.make_async_copy(sin_hbm, sin_ref, in_sem.at[8]),
    ]
    for load in loads:
        load.start()

    barrier = pltpu.get_barrier_semaphore()
    peers = [(right, head), (left, head), (partner, head)]
    peers += [(me, (head + j) % n_head) for j in range(1, n_head)]
    for peer in peers:
        pl.semaphore_signal(barrier, inc=1, device_id=peer, device_id_type=MESH)

    def part_of(p, w, owner):
        first, count = spans[p]
        return bufs[min(p, 1)].at[owner, pl.ds(w * piece + first, count)]

    def ring(p, w, s):
        ref = part_of(p, w, index_of(pos - signs[w] * s, core))
        return pltpu.make_async_remote_copy(
            ref, ref, rs.at[w * parts + p, s], rr.at[w * parts + p, s],
            device_id=(targets[w], head), device_id_type=MESH)

    def ring_in(p, w, s):
        ref = part_of(p, w, index_of(pos - signs[w] * (s + 1), core))
        return pltpu.make_async_remote_copy(
            ref, ref, rs.at[w * parts + p, s], rr.at[w * parts + p, s],
            device_id=(targets[w], head), device_id_type=MESH)

    def across(p, w, s, lane):
        ref = part_of(p, w, index_of(pos - signs[w] * s, lane))
        return pltpu.make_async_remote_copy(
            ref, ref, cs.at[w * parts + p, s], cr.at[w * parts + p, s],
            device_id=(partner, head), device_id_type=MESH)

    def relay(u, j):
        return pltpu.make_async_remote_copy(
            parcel.at[u, j - 1], arrived.at[u, j - 1], hs.at[u, j - 1], hr.at[u, j - 1],
            device_id=(me, (head + j) % n_head), device_id_type=MESH)

    shift = [(n_head - src_ref[k] // group) % n_head for k in range(group)]
    taken = [src_ref[k] % group for k in range(group)]
    slot = [
        sum([(shift[l] == shift[k]).astype(jnp.int32) for l in range(k)], jnp.int32(0))
        for k in range(group)
    ]

    def flag(cond):
        return jnp.where(cond, 1.0, 0.0).astype(jnp.float32)

    units = [w * 2 + half for half in range(2) for w in range(ways)]

    def weigh(u, weights):
        total = jnp.zeros((sub, hd), jnp.float32)
        for c_m in range(group):
            block = own_ref[u * sub:(u + 1) * sub, c_m * hd:(c_m + 1) * hd]
            total = total + block.astype(jnp.float32) * weights[c_m]
        return total.astype(jnp.bfloat16)

    for load in loads[:2]:
        load.wait()
    pl.semaphore_wait(barrier, len(peers))
    for w in range(ways):
        ring(0, w, 0).start()
    for w in range(ways):
        across(0, w, 0, core).start()
    for load in loads[2:4]:
        load.wait()
    for u in units:
        for j in range(1, n_head):
            for c in range(capacity):
                weights = [
                    sum([flag((shift[k] == j) & (slot[k] == c) & (taken[k] == c_m))
                         for k in range(group)], jnp.float32(0))
                    for c_m in range(group)
                ]
                parcel[u, j - 1, c] = weigh(u, weights)
            relay(u, j).start()
    for k in range(group):
        weights = [flag((shift[k] == 0) & (taken[k] == c_m)) for c_m in range(group)]
        for u in units:
            wq[me, u * sub:(u + 1) * sub, k * hd:(k + 1) * hd] = weigh(u, weights)
    for load in loads[4:]:
        load.wait()
    accq[...] = jnp.zeros_like(accq)
    acckv[...] = jnp.zeros_like(acckv)

    def add(p, w, owner):
        xs = x_ref[:, pl.ds(pl.multiple_of(owner * rows + w * piece, 128), piece)]
        acc = (acckv, accq)[p]
        acc[...] += dot(xs, bufs[p][owner, pl.ds(w * piece, piece), :], 1, 0)

    def pass_on(p, w, s):
        ring_in(p, w, s - 1).wait_recv()

        @pl.when(s < m - 1)
        def _():
            ring(p, w, s).start()

        across(p, w, s, core).start()

    def unit_out(u):
        block = pl.ds(u * sub, sub)
        for j in range(1, n_head):
            relay(u, j).wait_recv()
        for k in range(group):
            cols = slice(k * hd, (k + 1) * hd)
            total = wq[me, block, cols].astype(jnp.float32)
            for j in range(1, n_head):
                for c in range(capacity):
                    weight = flag((shift[k] == j) & (slot[k] == c))
                    total = total + arrived[u, j - 1, c].astype(jnp.float32) * weight
            wq[me, block, cols] = total.astype(jnp.bfloat16)
        ring(1 + u % 2, u // 2, 0).start()
        across(1 + u % 2, u // 2, 0, core).start()

    for w in range(ways):
        add(0, w, me)
    for u in units[:ways]:
        unit_out(u)
    for s in range(1, lead + 1):
        for w in range(ways):
            pass_on(0, w, s)
        if s == 1:
            for u in units[ways:]:
                unit_out(u)
    for w in range(ways):
        add(1, w, me)

    def step(s, carry):
        @pl.when(s + lead < m)
        def _():
            for w in range(ways):
                pass_on(0, w, s + lead)

        for p in range(1, parts):
            for w in range(ways):
                pass_on(p, w, s)
        for w in range(ways):
            for p in range(2):
                add(p, w, index_of(pos - signs[w] * s, core))
        for w in range(ways):
            for p in range(parts):
                across(p, w, s - 1, 1 - core).wait_recv()
        for w in range(ways):
            for p in range(2):
                add(p, w, index_of(pos - signs[w] * (s - 1), 1 - core))
        return carry

    lax.fori_loop(1, m, step, 0)
    for w in range(ways):
        for p in range(parts):
            across(p, w, m - 1, 1 - core).wait_recv()
        for p in range(2):
            add(p, w, index_of(pos - signs[w] * (m - 1), 1 - core))

    scale = 1.0 / math.sqrt(hd)
    cosine, sine = cos_ref[...], sin_ref[...]

    def rotate(f):
        return f * cosine + pltpu.roll(f, hd // 2, 1) * sine

    def rotate_back(f):
        return f * cosine - pltpu.roll(f, hd // 2, 1) * sine

    docs = jnp.broadcast_to(doc_ref[...].astype(jnp.float32), (length, length))
    at_key = lax.broadcasted_iota(jnp.int32, (length, length), 1)
    at_query = lax.broadcasted_iota(jnp.int32, (length, length), 0)
    allowed = (at_key <= at_query) & (docs == docs.T)
    key = rotate(acckv[:, :hd]).astype(jnp.bfloat16)
    value = acckv[:, hd:].astype(jnp.bfloat16)
    dkey = jnp.zeros((length, hd), jnp.float32)
    dvalue = jnp.zeros((length, hd), jnp.float32)
    for k in range(group):
        cols = slice(k * hd, (k + 1) * hd)
        query = rotate(accq[:, cols]).astype(jnp.bfloat16)
        given = g_ref[:, cols]
        scores = jnp.where(allowed, dot(query, key, 1, 1) * scale, neg_large)
        weights = jnp.exp(scores - jnp.max(scores, axis=-1, keepdims=True))
        probs = weights / jnp.sum(weights, axis=-1, keepdims=True)
        probs_b = probs.astype(jnp.bfloat16)
        out_ref[:, cols] = dot(probs_b, value, 1, 0).astype(jnp.bfloat16)
        prob_grad = dot(given, value, 1, 1)
        centre = jnp.sum(probs * prob_grad, axis=-1, keepdims=True)
        dscore = (probs * (prob_grad - centre) * scale).astype(jnp.bfloat16)
        dq_ref[:, cols] = rotate_back(dot(dscore, key, 1, 0)).astype(jnp.bfloat16)
        dkey = dkey + dot(dscore, query, 0, 0)
        dvalue = dvalue + dot(probs_b, given, 0, 0)
    dkv_ref[:, :hd] = rotate_back(dkey).astype(jnp.bfloat16)
    dkv_ref[:, hd:] = dvalue.astype(jnp.bfloat16)

    chunks = n_dp // n_head

    def partial(owner):
        return (dot(dq_ref[...], wq[owner], 1, 1) + dot(dkv_ref[...], wkv[owner], 1, 1)).astype(
            jnp.bfloat16)

    def share(j, i):
        return pltpu.make_async_remote_copy(
            psend.at[j - 1, i], precv.at[j - 1, i], ps.at[j - 1, i], pr.at[j - 1, i],
            device_id=(me, (head + j) % n_head), device_id_type=MESH)

    for j in range(1, n_head):
        def send_chunk(i, carry):
            psend[j - 1, i] = partial(((head + j) % n_head) * chunks + i)
            share(j, i).start()
            return carry

        lax.fori_loop(0, chunks, send_chunk, 0)

    def own_chunk(i, carry):
        cols = pl.ds(pl.multiple_of(i * rows, 128), rows)
        grad_ref[:, cols] = partial(head * chunks + i)
        return carry

    lax.fori_loop(0, chunks, own_chunk, 0)

    def finish(i, carry):
        cols = pl.ds(pl.multiple_of(i * rows, 128), rows)
        total = grad_ref[:, cols].astype(jnp.float32)
        for j in range(1, n_head):
            share(j, i).wait_recv()
            total = total + precv[j - 1, i].astype(jnp.float32)
        grad_ref[:, cols] = total.astype(jnp.bfloat16)
        return carry

    lax.fori_loop(0, chunks, finish, 0)

    def drain(s, carry):
        for p in range(parts):
            for w in range(ways):
                @pl.when(s < m - 1)
                def _():
                    ring(p, w, s).wait_send()

                across(p, w, s, core).wait_send()
        return carry

    lax.fori_loop(0, m, drain, 0)
    for j in range(1, n_head):
        for u in units:
            relay(u, j).wait_send()

        def drain_share(i, carry):
            share(j, i).wait_send()
            return carry

        lax.fori_loop(0, chunks, drain_share, 0)


def solution(mesh):
    n_dp, n_head = mesh.shape["dp"], mesh.shape["head"]

    def local(x, old, fresh, wk, wv, g, head_source, doc_ids):
        length, width = x.shape
        rows, hd = wk.shape
        group = g.shape[1] // hd
        ways = 2 if rows % 256 == 0 else 1
        m = n_dp // 2
        capacity = (group + n_head - 1) // n_head
        chunks = n_dp // n_head
        cosine, sine = rotary_tables(length, hd)
        bf, f32 = jnp.bfloat16, jnp.float32
        vm = pl.BlockSpec(memory_space=pltpu.VMEM)
        anyspace = pl.BlockSpec(memory_space=pl.ANY)
        dma = pltpu.SemaphoreType.DMA
        return pl.pallas_call(
            functools.partial(kernel, n_dp, n_head, group, ways),
            out_shape=(
                jax.ShapeDtypeStruct((length, group * hd), bf),
                jax.ShapeDtypeStruct((length, width // n_head), bf),
            ),
            in_specs=[pl.BlockSpec(memory_space=pltpu.SMEM)] + [anyspace] * 9,
            out_specs=(vm, vm),
            scratch_shapes=[
                pltpu.VMEM((1, length), jnp.int32),
                pltpu.VMEM((length, hd), f32),
                pltpu.VMEM((length, hd), f32),
                pltpu.VMEM((length, width), bf),
                pltpu.VMEM((rows, group * hd), bf),
                pltpu.VMEM((length, group * hd), bf),
                pltpu.VMEM((n_dp, rows, group * hd), bf),
                pltpu.VMEM((n_dp, rows, 2 * hd), bf),
                pltpu.VMEM((2 * ways, n_head - 1, capacity, rows // (2 * ways), hd), bf),
                pltpu.VMEM((2 * ways, n_head - 1, capacity, rows // (2 * ways), hd), bf),
                pltpu.VMEM((length, group * hd), f32),
                pltpu.VMEM((length, 2 * hd), f32),
                pltpu.VMEM((length, group * hd), bf),
                pltpu.VMEM((length, 2 * hd), bf),
                pltpu.VMEM((n_head - 1, chunks, length, rows), bf),
                pltpu.VMEM((n_head - 1, chunks, length, rows), bf),
                dma((9,)),
                dma((3 * ways, m)),
                dma((3 * ways, m)),
                dma((3 * ways, m)),
                dma((3 * ways, m)),
                dma((2 * ways, n_head - 1)),
                dma((2 * ways, n_head - 1)),
                dma((n_head - 1, chunks)),
                dma((n_head - 1, chunks)),
            ],
            compiler_params=pltpu.CompilerParams(
                collective_id=0, has_side_effects=True, vmem_limit_bytes=67043328),
        )(head_source, doc_ids.reshape(1, -1), cosine, sine, x, old, fresh, wk, wv, g)

    in_specs = (
        P("dp", None), P("dp", "head"), P("dp", "head"), P("dp", "head"),
        P("dp", "head"), P("dp", "head"), P(), P("dp"),
    )
    return jax.shard_map(
        local, mesh=mesh, in_specs=in_specs,
        out_specs=(P("dp", "head"), P("dp", "head")), check_vma=False)
```
